128 devices in a mesh: samp: 8 (over z, y_lo), feat: 16 (over x, y_hi, core).
Axes of the slice: x: 4, y: 4 (y_hi: 2, y_lo: 2; y = y_hi * 2 + y_lo), z: 4, core: 2. Of those that a mesh axis runs over, the one named last changes fastest.
Arguments:
- design: bfloat16 [12288, 8192], P('samp', 'feat'), may hold values from -6 to 6
- labels: int32 [12288], P('samp'), may hold values 0 or 1
- coef_all: float32 [1048576], replicated, may hold values from -0.13 to 0.13
- active: int32 [8192], P('feat'), may hold values from 0 to 1048575, as said below
- penalty: float32 [8192], P('feat'), may hold values from 4 to 40
Outputs:
- gram: float32 [8192, 8192], P('samp', 'feat')
- gradient: float32 [8192], P('feat')
The draws below stay inside these ranges and needn't reach their ends.
Inputs may be any that keep to these rules, and one draw needn't show every extreme that they name: `active`: the indices are distinct.
All inputs are finite; a program needn't handle non-finite values. No bound on the sum of `labels` on one device may be relied on, other than what follows from the above.
Results may differ from the reference program's by a relative error of at most 0.003.
Values may be sent and summed in bfloat16 or wider, within the bound.
No kernel may reach another device: no remote copies, remote signals or barrier semaphores. Data moves between devices by JAX's collectives and lax.ppermute only.
A program may use at most 128 MiB of HBM per device.

```python
import math
import jax
import jax.numpy as jnp
from jax import lax

A = 8192
POOL = 1048576
N = 12288


def draw_active(key, part):
    return jax.random.permutation(key, POOL)[:A].astype(jnp.int32)


def with_ends(array, stream_key, smallest, high):
    place = [jax.random.randint(jax.random.fold_in(stream_key, axis), (), 0, length) for axis, length in enumerate(array.shape)]
    widest = array.shape.index(max(array.shape))
    beside = place[:widest] + [(place[widest] + 1) % array.shape[widest]] + place[widest + 1:]
    return array.at[tuple(place)].set(smallest).at[tuple(beside)].set(high)


def block_levels(key, extent, split, least, top_value):
    def one(axis_at, blocks):
        heights = jax.random.uniform(jax.random.fold_in(jax.random.fold_in(key, 6), axis_at), (blocks,), jnp.float32, least / len(split), top_value / len(split))
        return jnp.repeat(jnp.exp(heights), extent[axis_at] // blocks).reshape((-1,) + (1,) * (len(extent) - axis_at - 1))

    loudness = one(*split[0])
    for cut in split[1:]:
        loudness = loudness * one(*cut)
    return loudness


def normal_values(own_key, dims, spread, reach, shards=(), kind=jnp.bfloat16):
    entries = jax.random.normal(own_key, dims, jnp.float32) * spread
    if len(shards) > 0:
        entries = block_levels(own_key, dims, shards, -0.22, 0.18) * entries
    return jnp.clip(entries, min=-reach, max=reach).astype(kind)


def setup_inputs(seed: int = 0) -> dict:
    splits = jax.random.split(jax.random.key(seed), 6)
    design = normal_values(splits[0], (N, A), 1.0, 6.0, ((0, 8), (1, 16)))
    labels = with_ends((jax.random.randint(splits[1], (N,), 0, 2) < 1).astype(jnp.int32), jax.random.fold_in(splits[1], 1), 0, 1)
    coef_all = normal_values(splits[2], (POOL,), 0.022, 0.13, (), jnp.float32)
    active = draw_active(jax.random.fold_in(splits[5], 71), 0)
    penalty = jnp.clip(jnp.exp(math.log(40.0) - 2.3025851 * jax.random.uniform(splits[4], (A,), jnp.float32) ** block_levels(splits[4], (A,), ((0, 16),), -0.2, 0.2)), 4.0, 40.0)
    return dict(design=design, labels=labels, coef_all=coef_all, active=active, penalty=penalty)


def reference(design, labels, coef_all, active, penalty):
    beta = coef_all[active]
    beta_b = beta.astype(jnp.bfloat16)
    margin = jnp.dot(design, beta_b, preferred_element_type=jnp.float32)
    prob = 1.0 / (1.0 + jnp.exp(-margin))
    weight = prob * (1.0 - prob)
    resid = prob - labels.astype(jnp.float32)
    weighted = (design.astype(jnp.float32) * weight[:, None]).astype(jnp.bfloat16)
    resid_b = resid.astype(jnp.bfloat16)
    scale = 1.0 / jnp.sqrt(jnp.float32(N))
    gram = lax.dot_general(design.astype(jnp.float32), weighted.astype(jnp.float32), (((0,), (0,)), ((), ())), preferred_element_type=jnp.float32) * scale
    grad_data = jnp.dot(resid_b, design, preferred_element_type=jnp.float32) * scale
    gradient = grad_data + penalty * beta
    return (gram, gradient)
```

```python
import itertools

import jax
import jax.numpy as jnp
from jax import lax
from jax.sharding import Mesh
from jax.sharding import PartitionSpec as P

AXES = ("z", "l", "x", "h", "c")
SAMP = ("z", "l")
FEAT = ("x", "h", "c")
SIZES = (4, 2, 4, 2, 2)
F32 = jnp.float32
BF16 = jnp.bfloat16


def send(value, route):
    pairs = []
    for source, at in enumerate(itertools.product(*map(range, SIZES))):
        target = route(*at)
        if target is not None:
            index = 0
            for size, place in zip(SIZES, target):
                index = index * size + place % size
            pairs.append((source, index))
    return lax.ppermute(value, AXES, pairs)


def core_swap(value):
    return send(value, lambda z, l, x, h, c: (z, l, x, h, 1 - c))


def near_route(z, l, x, h, c):
    return (z ^ 1 if c == 0 else 3 - z, l, x, h, c)


def over_route(z, l, x, h, c):
    return (3 - z if c == 0 else z ^ 1, l, x, h, c)


def sum_over_l(same, other, keeps):
    swapped = send(
        jnp.where(keeps, other, same).astype(BF16),
        lambda z, l, x, h, c: (z, h, x, 1 - h, c) if l == h else (z, h, x, h, c),
    )
    over = send(other.astype(BF16), lambda z, l, x, h, c: None if l == h else (z, h, x, 1 - h, c))
    return jnp.where(keeps, same, over.astype(F32)) + swapped.astype(F32)


def product(rows, weighted):
    return lax.dot_general(
        rows, weighted, (((0,), (0,)), ((), ())), preferred_element_type=F32
    ).astype(BF16)


def per_device(design, labels, coef_all, active, penalty):
    z, l, x, h, c = (lax.axis_index(name) for name in AXES)
    scale = 1.0 / jnp.sqrt(F32(design.shape[0] * 8))
    across = core_swap(design)
    beta = coef_all[active]
    part = jnp.dot(design, beta.astype(BF16), preferred_element_type=F32)
    part = part + core_swap(part)
    part = part + send(part, lambda z, l, x, h, c: (z, l, x, 1 - h, c))
    part = part + send(part, lambda z, l, x, h, c: (z, l, x ^ 1, h, c))
    margin = part + send(part, lambda z, l, x, h, c: (z, l, 3 - x, h, c))
    beside = send(design, lambda z, l, x, h, c: (z, l, x, 1 - h, c))
    ahead = send(design, lambda z, l, x, h, c: (z, l, x - 1, h, c))
    behind = send(design, lambda z, l, x, h, c: (z, l, x + 1, h, c))
    prob = 1.0 / (1.0 + jnp.exp(-margin))
    weight = prob * (1.0 - prob)
    resid_b = (prob - labels.astype(F32)).astype(BF16)
    grad = jnp.dot(resid_b, design, preferred_element_type=F32)
    grad = grad + send(grad, near_route)
    grad = grad + send(grad, over_route)
    grad = grad + send(grad, lambda z, l, x, h, c: (z, 1 - l, x, h, c))
    gradient = grad * scale + penalty * beta

    def weigh(block):
        return (block.astype(F32) * weight[:, None]).astype(BF16)

    both = lax.optimization_barrier(jnp.concatenate([weigh(design), weigh(beside)], axis=1))
    far = send(jnp.where(c == 0, behind, ahead), lambda z, l, x, h, c: (z, l, x + 1 - 2 * c, h, c))
    blocks = {
        0: (design, across),
        1: (ahead, core_swap(ahead)),
        3: (behind, core_swap(behind)),
        2: (far, core_swap(far)),
    }
    terms = [[product(blocks[j][r], both) for j in range(4)] for r in range(2)]

    def pick(r, place):
        j = (place - x) % 4
        first = jnp.where(j == 1, terms[r][1], terms[r][0])
        second = jnp.where(j == 3, terms[r][3], terms[r][2])
        return jnp.where(j >= 2, second, first)

    near = jnp.where(c == 0, z ^ 1, 3 - z)
    over = jnp.where(c == 0, 3 - z, z ^ 1)
    outs = []
    for r in range(2):
        far_side = send(pick(r, z ^ 2), near_route)
        near_side = send(pick(r, near), near_route)
        passed = pick(r, over).astype(F32) + far_side.astype(F32)
        over_side = send(passed.astype(BF16), over_route)
        total = pick(r, z).astype(F32) + near_side.astype(F32) + over_side.astype(F32)
        outs.append(sum_over_l(total[:, :512], total[:, 512:], l == h) * scale)
    first = jnp.where(c == 0, outs[0], outs[1])
    second = jnp.where(c == 0, outs[1], outs[0])
    return (jnp.concatenate([first, second], axis=0), gradient)


def solution(mesh):
    split = Mesh(mesh.devices.reshape(SIZES), AXES)
    placed = (P(SAMP, FEAT), P(SAMP), P(), P(FEAT), P(FEAT))

    return jax.shard_map(
        per_device, mesh=split, in_specs=placed, out_specs=(P(SAMP, FEAT), P(FEAT)), check_vma=False
    )
```

```python
import itertools

import jax
import jax.numpy as jnp
from jax import lax
from jax.sharding import Mesh
from jax.sharding import PartitionSpec as P

AXES = ("z", "l", "x", "h", "c")
SAMP = ("z", "l")
FEAT = ("x", "h", "c")
SIZES = (4, 2, 4, 2, 2)
F32 = jnp.float32
BF16 = jnp.bfloat16


def send(value, route):
    pairs = []
    for source, at in enumerate(itertools.product(*map(range, SIZES))):
        target = route(*at)
        if target is not None:
            index = 0
            for size, place in zip(SIZES, target):
                index = index * size + place % size
            pairs.append((source, index))
    return lax.ppermute(value, AXES, pairs)


def core_swap(value):
    return send(value, lambda z, l, x, h, c: (z, l, x, h, 1 - c))


def other_h(z, l, x, h, c):
    return (z, l, x, 1 - h, c)


def near_route(z, l, x, h, c):
    return (z ^ 1 if c == 0 else 3 - z, l, x, h, c)


def over_route(z, l, x, h, c):
    return (3 - z if c == 0 else z ^ 1, l, x, h, c)


def with_ring(z, l, x, h, c):
    return (z, l, x + 1 - 2 * c, h, c)


def against_ring(z, l, x, h, c):
    return (z, l, x - 1 + 2 * c, h, c)


def sum_over_l(same, other, keeps):
    there = send(other.astype(BF16), lambda z, l, x, h, c: (z, 1 - l, x, 1 - h, c))
    back = send(
        jnp.where(keeps, there, same.astype(BF16)), lambda z, l, x, h, c: (z, 1 - l, x, h, c)
    )
    return jnp.where(keeps, same.astype(F32), there.astype(F32)) + back.astype(F32)


def product(rows, weighted):
    return lax.dot_general(
        rows, weighted, (((0,), (0,)), ((), ())), preferred_element_type=F32
    ).astype(BF16)


def per_device(design, labels, coef_all, active, penalty):
    z, l, x, h, c = (lax.axis_index(name) for name in AXES)
    keeps = l == h
    scale = 1.0 / jnp.sqrt(F32(design.shape[0] * 8))
    half = design.shape[1] // 2

    def halves(array):
        return array[:, :half], array[:, half:]

    mine = [lax.optimization_barrier(half_of) for half_of in halves(design)]
    first = send(design, with_ring)
    far = [send(lax.optimization_barrier(halves(first)[k]), with_ring) for k in range(2)]
    second = [send(mine[k], against_ring) for k in range(2)]
    beside = send(design, other_h)
    across = core_swap(design)
    beta = coef_all[active]
    part = jnp.dot(design, beta.astype(BF16), preferred_element_type=F32)
    part = part + send(part, other_h)
    one = send(part, against_ring)
    two = send(one, against_ring)
    part = part + one + two + send(two, against_ring)
    margin = part + core_swap(part)
    prob = 1.0 / (1.0 + jnp.exp(-margin))
    weight = prob * (1.0 - prob)
    resid_b = (prob - labels.astype(F32)).astype(BF16)
    grad = jnp.dot(resid_b, design, preferred_element_type=F32)
    grad = grad + send(grad, near_route)
    grad = grad + send(grad, over_route)
    grad = grad + send(grad, lambda z, l, x, h, c: (z, 1 - l, x, h, c))
    gradient = grad * scale + penalty * beta

    def weigh(block):
        return (block.astype(F32) * weight[:, None]).astype(BF16)

    first_across = core_swap(first)
    far_across = [core_swap(far[k]) for k in range(2)]
    second_across = [core_swap(second[k]) for k in range(2)]
    places = {
        "q": z ^ 2,
        "p": jnp.where(c == 0, z ^ 1, 3 - z),
        "s": jnp.where(c == 0, 3 - z, z ^ 1),
        "z": z,
    }

    def pick(*block):
        return lax.optimization_barrier(jnp.stack(block))

    def rows_of(k):
        own = pick(mine[k], second[k], far[k], halves(first)[k])
        other = pick(
            halves(across)[k], halves(first_across)[k], far_across[k], second_across[k]
        )
        return own, other

    own, other = [None, None], [None, None]
    own[0], other[0] = rows_of(0)
    beside, own[0], other[0] = lax.optimization_barrier((beside, own[0], other[0]))
    both = jnp.concatenate([weigh(design), weigh(beside)], axis=1)
    both, far[1], second[1] = lax.optimization_barrier((both, far[1], second[1]))
    own[1], other[1] = rows_of(1)

    def products(rows):
        def at(place):
            j = ((place - x) * (1 - 2 * c)) % 4
            return product(lax.dynamic_index_in_dim(rows, j, 0, keepdims=False), both)

        return {name: at(place) for name, place in places.items()}

    def sum_over_z(terms):
        far_side = send(terms["q"].astype(BF16), near_route)
        near_side = send(terms["p"].astype(BF16), near_route)
        passed = terms["s"].astype(F32) + far_side.astype(F32)
        over_side = send(passed.astype(BF16), over_route)
        return terms["z"].astype(F32) + near_side.astype(F32) + over_side.astype(F32)

    width = design.shape[1]
    terms = products(own[0])
    joined = jnp.concatenate(list(terms.values()), axis=0)
    summed = sum_over_l(joined[:, :width], joined[:, width:], keeps)
    blocks = [sum_over_z(dict(zip(terms, jnp.split(summed, 4))))]
    for rows in (other[0], own[1], other[1]):
        total = sum_over_z(products(rows))
        blocks.append(sum_over_l(total[:, :width], total[:, width:], keeps))
    ours = jnp.concatenate([blocks[0], blocks[2]], axis=0) * scale
    theirs = jnp.concatenate([blocks[1], blocks[3]], axis=0) * scale
    top = jnp.where(c == 0, ours, theirs)
    low = jnp.where(c == 0, theirs, ours)
    return (jnp.concatenate([top, low], axis=0), gradient)


def solution(mesh):
    split = Mesh(mesh.devices.reshape(SIZES), AXES)
    placed = (P(SAMP, FEAT), P(SAMP), P(), P(FEAT), P(FEAT))

    return jax.shard_map(
        per_device, mesh=split, in_specs=placed, out_specs=(P(SAMP, FEAT), P(FEAT)), check_vma=False
    )
```

```python
import itertools

import jax
import jax.numpy as jnp
from jax import lax
from jax.sharding import Mesh
from jax.sharding import PartitionSpec as P

AXES = ("z", "l", "x", "h", "c")
SAMP = ("z", "l")
FEAT = ("x", "h", "c")
SIZES = (4, 2, 4, 2, 2)
F32 = jnp.float32
BF16 = jnp.bfloat16


def send(value, route):
    pairs = []
    for source, at in enumerate(itertools.product(*map(range, SIZES))):
        target = route(*at)
        if target is not None:
            index = 0
            for size, place in zip(SIZES, target):
                index = index * size + place % size
            pairs.append((source, index))
    return lax.ppermute(value, AXES, pairs)


def core_swap(value):
    return send(value, lambda z, l, x, h, c: (z, l, x, h, 1 - c))


def with_y(z, l, x, h, c):
    y = 2 * h + l + 1 - 2 * c
    return (z, y % 2, x, y // 2 % 2, c)


def against_y(z, l, x, h, c):
    y = 2 * h + l - 1 + 2 * c
    return (z, y % 2, x, y // 2 % 2, c)


def near_route(z, l, x, h, c):
    return (z ^ 1 if c == 0 else 3 - z, l, x, h, c)


def over_route(z, l, x, h, c):
    return (3 - z if c == 0 else z ^ 1, l, x, h, c)


def with_ring(z, l, x, h, c):
    return (z, l, x + 1 - 2 * c, h, c)


def against_ring(z, l, x, h, c):
    return (z, l, x - 1 + 2 * c, h, c)


def sum_over_l(same, other, keeps, tail=None):
    there = send(other.astype(BF16), lambda z, l, x, h, c: (z, 1 - l, x, 1 - h, c))
    back = jnp.where(keeps, there, same.astype(BF16))
    if tail is not None:
        back = with_tail(back, tail)
    back = send(back, lambda z, l, x, h, c: (z, 1 - l, x, h, c))
    return same, there, back


def joined_sum(keeps, same, there, back):
    return jnp.where(keeps, same.astype(F32), there.astype(F32)) + back.astype(F32)


def with_tail(block, tail):
    high = lax.reduce_precision(tail, 8, 7)
    row = jnp.concatenate([high, tail - high]).astype(BF16).reshape(-1, block.shape[1])
    return jnp.concatenate([block, jnp.pad(row, ((0, 16 - row.shape[0]), (0, 0)))], axis=0)


def split_tail(block, length):
    row = block[-16:].reshape(-1)[: 2 * length].astype(F32)
    return block[:-16], row[:length] + row[length:]


def product(rows, weighted):
    return lax.dot_general(
        rows, weighted, (((0,), (0,)), ((), ())), preferred_element_type=F32
    ).astype(BF16)


def per_device(design, labels, coef_all, active, penalty):
    z, l, x, h, c = (lax.axis_index(name) for name in AXES)
    keeps = l == h
    scale = 1.0 / jnp.sqrt(F32(design.shape[0] * 8))
    half = design.shape[1] // 2

    def halves(array):
        return array[:, :half], array[:, half:]

    first = send(design, with_ring)
    beside = send(send(design, with_y), with_y)
    across = core_swap(design)
    beta = coef_all[active]
    part = jnp.dot(design, beta.astype(BF16), preferred_element_type=F32)
    part = part + send(send(part, against_y), against_y)
    one = send(part, against_ring)
    two = send(one, against_ring)
    part = part + one + two + send(two, against_ring)
    mine = [None, None]
    second = [None, None]
    far = [None, None]
    mine[0], _ = lax.optimization_barrier((design[:, :half], one))
    second[0] = send(mine[0], against_ring)
    far[0] = send(lax.optimization_barrier(first[:, :half]), with_ring)
    mine[1] = lax.optimization_barrier((design, part))[0][:, half:]
    second[1] = send(mine[1], against_ring)
    first_late = lax.optimization_barrier((first, part))[0][:, half:]
    far[1] = send(first_late, with_ring)
    margin = part + core_swap(part)
    prob = 1.0 / (1.0 + jnp.exp(-margin))
    weight = prob * (1.0 - prob)
    resid_b = (prob - labels.astype(F32)).astype(BF16)
    grad = jnp.dot(resid_b, design, preferred_element_type=F32)

    def weigh(block):
        return (block.astype(F32) * weight[:, None]).astype(BF16)

    places = {
        "q": z ^ 2,
        "p": jnp.where(c == 0, z ^ 1, 3 - z),
        "s": jnp.where(c == 0, 3 - z, z ^ 1),
        "z": z,
    }

    def pick(*block):
        return lax.optimization_barrier(jnp.stack(block))

    first_across = core_swap(first)

    def rows_of(k):
        own = pick(mine[k], second[k], far[k], halves(first)[k])
        other = pick(
            halves(across)[k], halves(first_across)[k], core_swap(far[k]), core_swap(second[k])
        )
        return own, other

    rows_y, rows_p = rows_of(0)
    beside, rows_y = lax.optimization_barrier((beside, rows_y))
    both = jnp.concatenate([weigh(design), weigh(beside)], axis=1)
    both = lax.optimization_barrier(both)

    def products(rows):
        def at(name):
            j = ((places[name] - x) * (1 - 2 * c)) % 4
            return product(lax.dynamic_index_in_dim(rows, j, 0, keepdims=False), both)

        return {name: at(name) for name in "qpsz"}

    def sum_over_z(terms, tail=None):
        near_side = send(terms["p"].astype(BF16), near_route)
        far_side = send(terms["q"], near_route)
        if tail is not None:
            far_side, more = split_tail(far_side, tail.shape[0])
            tail = tail + more
        passed = (terms["s"].astype(F32) + far_side.astype(F32)).astype(BF16)
        if tail is not None:
            passed = with_tail(passed, tail)
        over_side = send(passed, over_route)
        if tail is not None:
            over_side, more = split_tail(over_side, tail.shape[0])
            tail = tail + more
        return terms["z"].astype(F32) + near_side.astype(F32) + over_side.astype(F32), tail

    width = design.shape[1]
    terms = products(rows_y)
    joined = jnp.concatenate(list(terms.values()), axis=0)
    rows_p, _ = lax.optimization_barrier((rows_p, joined))
    summed = joined_sum(keeps, *sum_over_l(joined[:, :width], joined[:, width:], keeps))
    terms = dict(zip(terms, jnp.split(summed, 4)))
    terms["q"] = terms["q"].astype(BF16)
    block_y, _ = sum_over_z(terms)
    terms = products(rows_p)
    terms["q"] = with_tail(terms["q"], grad)
    far[1], second[1], _, _ = lax.optimization_barrier(
        (far[1], second[1], terms["q"], terms["p"])
    )
    total, grad = sum_over_z(terms, grad)
    sums_p = sum_over_l(total[:, :width], total[:, width:], keeps, grad)
    rows_o, rows_q = rows_of(1)
    total, _ = sum_over_z(products(rows_o))
    sums_o = sum_over_l(total[:, :width], total[:, width:], keeps)
    total, _ = sum_over_z(products(rows_q))
    sums_q = sum_over_l(total[:, :width], total[:, width:], keeps)
    back_p, back_o, _ = lax.optimization_barrier((sums_p[2], sums_o[2], sums_q[2]))
    back_p, more = split_tail(back_p, grad.shape[0])
    gradient = (grad + more) * scale + penalty * beta
    blocks = [
        block_y,
        joined_sum(keeps, *sums_p[:2], back_p),
        joined_sum(keeps, *sums_o[:2], back_o),
        joined_sum(keeps, *sums_q),
    ]
    ours = jnp.concatenate([blocks[0], blocks[2]], axis=0) * scale
    theirs = jnp.concatenate([blocks[1], blocks[3]], axis=0) * scale
    top = jnp.where(c == 0, ours, theirs)
    low = jnp.where(c == 0, theirs, ours)
    return (jnp.concatenate([top, low], axis=0), gradient)


def solution(mesh):
    split = Mesh(mesh.devices.reshape(SIZES), AXES)
    placed = (P(SAMP, FEAT), P(SAMP), P(), P(FEAT), P(FEAT))

    return jax.shard_map(
        per_device, mesh=split, in_specs=placed, out_specs=(P(SAMP, FEAT), P(FEAT)), check_vma=False
    )
```
